512 devices in a mesh: seq: 16 (over z_lo, core), head: 32 (over z_hi, x, y).
Axes of the slice: x: 4, y: 4, z: 16 (z_hi: 2, z_lo: 8; z = z_hi * 8 + z_lo), core: 2. Of those that a mesh axis runs over, the one named last changes fastest.
Arguments:
- queries: bfloat16 [1024, 16384], P('seq', 'head'), may hold values from -8 to 8
- new_keys: bfloat16 [1024, 1024], P('seq'), may hold values from -6 to 6
- new_values: bfloat16 [1024, 1024], P('seq'), may hold values from -6 to 6
- cache_keys: bfloat16 [12288, 1024], P('seq'), may hold values from -8 to 8
- cache_values: bfloat16 [12288, 1024], P('seq'), may hold values from -6 to 6
- positions: int32 [1024], replicated, may hold values from 0 to 1023, each once
- cache_len: int32 [16], replicated, may hold values from 1 to 768, 7680 in all
- out_weight: bfloat16 [16384, 16384], P('head', 'seq'), may hold values from -3.5 to 3.5
Outputs:
- output: float32 [1024, 16384], P(None, 'seq')
The draws below stay inside these ranges and needn't reach their ends.
Inputs may be any that keep to these rules, and one draw needn't show every extreme that they name: A permutation of the block's positions 0 to 1023. `cache_len`: entry s is the number of live slots at the start of sequence group s's 768 cache slots; later slots of that group are not attended. Some group is full.
All inputs are finite; a program needn't handle non-finite values.
Results may differ from the reference program's by a relative error of at most 0.009.
Values may be sent and summed in bfloat16 or wider, within the bound.
No kernel may reach another device: no remote copies, remote signals or barrier semaphores. Data moves between devices by JAX's collectives and lax.ppermute only.
A program may use at most 128 MiB of HBM per device.

```python
import math
import jax
import jax.numpy as jnp
import numpy as np
from jax import lax

D = 16384
DH = 128
GQA = 16
CSTR = 768
H = 128
KVH = 8
TOKENS = 1024
CACHE = 12288
N_SEQ = 16


def draw_queries(key, part):
    base = jax.random.truncated_normal(jax.random.fold_in(key, 11), -8.0, 8.0, (TOKENS, H * DH), jnp.float32)
    return base.astype(jnp.bfloat16)


def draw_cache_keys(key, part):
    base = jax.random.truncated_normal(jax.random.fold_in(key, 23), -8.0, 8.0, (CACHE, KVH * DH), jnp.float32)
    return base.astype(jnp.bfloat16)


def shard_levels(stream_key, extent, pieces, smallest, top_value):
    def one(position, shards_of):
        heights = jax.random.uniform(jax.random.fold_in(jax.random.fold_in(stream_key, 6), position), (shards_of,), jnp.float32, smallest / len(pieces), top_value / len(pieces))
        return jnp.repeat(jnp.exp(heights), extent[position] // shards_of).reshape((-1,) + (1,) * (len(extent) - position - 1))

    level = one(*pieces[0])
    for cut in pieces[1:]:
        level = level * one(*cut)
    return level


def profile(amount, total, most, slope):
    portions = [(1 << 20) // math.isqrt(grade ** slope) + 1 for grade in range(2, amount + 1)]
    spare, counts = total - most - (amount - 1), [1] * (amount - 1)
    while spare > 0:
        free = [i for i in range(amount - 1) if counts[i] < most]
        mass, left = sum([portions[i] for i in free]), spare
        for i in free:
            addition = min(most - counts[i], max(1, left * portions[i] // mass), spare)
            counts[i] = counts[i] + addition
            spare = spare - addition
    return np.array([most] + counts)


def ragged(rng, number_of, total, reach, slope):
    if number_of == 2:
        one = jax.random.randint(rng, (), max(1, total - reach), min(reach, total - 1) + 1)
        return jnp.stack([one, total - one])
    sizes = jnp.asarray(profile(number_of, total, reach, slope), jnp.int32)
    couples = (number_of - 1) // 2
    source_of, taker = sizes[1:1 + 2 * couples:2], sizes[2:2 + 2 * couples:2]
    slack = jnp.minimum(source_of - 1, reach - taker)
    passed = jax.random.randint(jax.random.fold_in(rng, 1), (couples,), 0, 1 << 20) % (slack + 1)
    sizes = sizes.at[1:1 + 2 * couples:2].set(source_of - passed).at[2:2 + 2 * couples:2].set(taker + passed)
    return sizes[jax.random.permutation(jax.random.fold_in(rng, 2), number_of)]


def normal_values(stream_key, extent, scale, bound, pieces=(), kind=jnp.bfloat16):
    drawn = jax.random.normal(stream_key, extent, jnp.float32) * scale
    if len(pieces) > 0:
        drawn = shard_levels(stream_key, extent, pieces, -0.22, 0.18) * drawn
    return jnp.clip(drawn, min=-bound, max=bound).astype(kind)


def setup_inputs(seed: int = 0) -> dict:
    key_list = jax.random.split(jax.random.key(seed), 9)
    return {
        "queries": draw_queries(jax.random.fold_in(key_list[8], 71), 0),
        "new_keys": normal_values(key_list[1], (TOKENS, KVH * DH), 1.0, 6.0, ((0, 16),)),
        "new_values": normal_values(key_list[2], (TOKENS, KVH * DH), 1.0, 6.0, ((0, 16),)),
        "cache_keys": draw_cache_keys(jax.random.fold_in(key_list[8], 71), 0),
        "cache_values": normal_values(key_list[4], (CACHE, KVH * DH), 1.0, 6.0, ((0, 16),)),
        "positions": jax.random.permutation(key_list[5], TOKENS).astype(jnp.int32),
        "cache_len": ragged(key_list[6], N_SEQ, CACHE * 5 // 8, CSTR, 2).astype(jnp.int32),
        "out_weight": normal_values(key_list[7], (H * DH, D), (H * DH * 3 // (CACHE + TOKENS)) ** -0.5, 3.5, ((0, 32), (1, 16))),
    }


def reference(queries, new_keys, new_values, cache_keys, cache_values, positions, cache_len, out_weight):
    slots = jnp.arange(CACHE, dtype=jnp.int32)
    live = (slots % CSTR) < jnp.repeat(cache_len, CSTR, total_repeat_length=CACHE)
    causal = positions[None, :] <= positions[:, None]
    shown = jnp.concatenate([jnp.broadcast_to(live[None, :], (TOKENS, CACHE)), causal], axis=1)
    all_keys = jnp.concatenate([cache_keys, new_keys], axis=0)
    all_values = jnp.concatenate([cache_values, new_values], axis=0)

    def one_head(head):
        group = head // GQA
        query = lax.dynamic_slice_in_dim(queries, (head * DH).astype(jnp.int32), DH, 1)
        key_cols = lax.dynamic_slice_in_dim(all_keys, (group * DH).astype(jnp.int32), DH, 1)
        value_cols = lax.dynamic_slice_in_dim(all_values, (group * DH).astype(jnp.int32), DH, 1)
        scores = jnp.dot(query, key_cols.T, preferred_element_type=jnp.float32) * (DH ** -0.5)
        scores = jnp.where(shown, scores, -1e30)
        peak = jnp.max(scores, axis=1, keepdims=True)
        expo = jnp.where(shown, jnp.exp(scores - peak), 0.0)
        weight_sum = jnp.sum(expo, axis=1)
        mixed = jnp.dot(expo.astype(jnp.bfloat16), value_cols, preferred_element_type=jnp.float32)
        return (mixed / weight_sum[:, None]).astype(jnp.bfloat16)

    heads = lax.map(one_head, jnp.arange(H, dtype=jnp.int32))
    attended = jnp.transpose(heads, (1, 0, 2)).reshape(TOKENS, H * DH)
    return jnp.dot(attended, out_weight, preferred_element_type=jnp.float32)
```

```python
import functools

import jax
import jax.numpy as jnp
from jax import lax
from jax.experimental import pallas as pl
from jax.experimental.pallas import tpu as pltpu
from jax.sharding import Mesh
from jax.sharding import PartitionSpec as P

DH = 128
GQA = 16
LINE = "line"
NEAR = "near"
PAIR = "core"
FAR = "far"
PLANE = ("x", "y")
SEQ = (LINE, NEAR, PAIR)
HEAD = (FAR, *PLANE)
HIDDEN = -1e30
SCALE = DH**-0.5 * 1.4426950408889634
BF16 = jnp.bfloat16
F32 = jnp.float32


def sent_to_all(x, axes):
    copies = jnp.broadcast_to(x, (lax.axis_size(axes), *x.shape))
    return lax.all_to_all(copies, axes, split_axis=0, concat_axis=0, tiled=True)


def attend_kernel(lens_ref, key_pos_ref, query_pos_ref, query_ref, kv_ref, near_kv_ref, out_ref):
    lines, rows, width = query_ref.shape
    heads = width // DH
    tokens = lines * rows
    slices = [ref.at[core] for ref in (kv_ref, near_kv_ref) for core in range(2)]
    stripe = kv_ref.shape[1] - key_pos_ref.shape[1] // len(slices)
    nt = (((1,), (1,)), ((), ()))
    slot = lax.broadcasted_iota(jnp.int32, (1, stripe), 1)
    live = [slot < lens_ref[i] for i in range(len(slices))]
    causal = key_pos_ref[...] <= query_pos_ref[...]
    new_keys = jnp.concatenate([ref[stripe:, :DH] for ref in slices], axis=0)
    new_values = jnp.concatenate([ref[stripe:, DH:] for ref in slices], axis=0)
    lane = lax.broadcasted_iota(jnp.int32, (tokens, DH), 1)
    stats = jnp.zeros((tokens, DH), F32)
    for head in range(heads):
        query = query_ref[:, :, head * DH : (head + 1) * DH].reshape(tokens, DH)
        parts = [
            jnp.where(
                shown,
                lax.dot_general(query, ref[:stripe, :DH], nt, preferred_element_type=F32),
                HIDDEN,
            )
            for shown, ref in zip(live, slices)
        ]
        parts.append(
            jnp.where(
                causal, lax.dot_general(query, new_keys, nt, preferred_element_type=F32), HIDDEN
            )
        )
        peak = functools.reduce(
            jnp.maximum, [jnp.max(part, axis=1, keepdims=True) for part in parts]
        )
        peak = peak.astype(BF16).astype(F32)
        expo = [jnp.exp2((part - peak) * SCALE) for part in parts]
        total = sum(jnp.sum(part, axis=1, keepdims=True) for part in expo)
        values = [ref[:stripe, DH:] for ref in slices] + [new_values]
        mixed = sum(
            jnp.dot(part.astype(BF16), value, preferred_element_type=F32)
            for part, value in zip(expo, values)
        )
        out_ref[:, :, head * DH : (head + 1) * DH] = mixed.astype(BF16).reshape(lines, rows, DH)
        coarse = total.astype(BF16).astype(F32)
        stats = jnp.where(lane == head, peak, stats)
        stats = jnp.where(lane == heads + head, coarse, stats)
        stats = jnp.where(lane == 2 * heads + head, total - coarse, stats)
    out_ref[:, :, width:] = stats.astype(BF16).reshape(lines, rows, DH)


def attend(lens, key_pos, query_pos, queries, kv, near_kv):
    lines, rows, width = queries.shape
    work = lines * rows * (width // DH) * 4 * kv.shape[1]
    vmem = pl.BlockSpec(memory_space=pltpu.VMEM)
    return pl.pallas_call(
        attend_kernel,
        out_shape=jax.ShapeDtypeStruct((lines, rows, width + DH), BF16),
        in_specs=[pl.BlockSpec(memory_space=pltpu.SMEM), vmem, vmem, vmem, vmem, vmem],
        out_specs=vmem,
        compiler_params=pltpu.CompilerParams(vmem_limit_bytes=40 << 20),
        cost_estimate=pl.CostEstimate(
            flops=4 * work * DH, transcendentals=work, bytes_accessed=4 * (queries.size + kv.size)
        ),
        name="attend",
    )(lens, key_pos, query_pos, queries, kv, near_kv)


def combine_kernel(part_ref, out_ref):
    width = out_ref.shape[1]
    heads = width // DH
    stats = part_ref[:, :, width:].astype(F32)
    for head in range(heads):
        peaks = stats[:, :, head : head + 1]
        sums = (
            stats[:, :, heads + head : heads + head + 1]
            + stats[:, :, 2 * heads + head : 2 * heads + head + 1]
        )
        scale = jnp.exp2((peaks - jnp.max(peaks, axis=0, keepdims=True)) * SCALE)
        scale = scale / jnp.sum(scale * sums, axis=0, keepdims=True)
        columns = slice(head * DH, (head + 1) * DH)
        mixed = jnp.sum(part_ref[:, :, columns].astype(F32) * scale, axis=0)
        out_ref[:, columns] = mixed.astype(BF16)


def combine(parts):
    lines, rows, width = parts.shape
    vmem = pl.BlockSpec(memory_space=pltpu.VMEM)
    return pl.pallas_call(
        combine_kernel,
        out_shape=jax.ShapeDtypeStruct((rows, width - DH), BF16),
        in_specs=[vmem],
        out_specs=vmem,
        cost_estimate=pl.CostEstimate(
            flops=2 * parts.size, transcendentals=0, bytes_accessed=2 * parts.size
        ),
        name="combine",
    )(parts)


def body(queries, new_keys, new_values, cache_keys, cache_values, positions, cache_len, out_weight):
    tok_dev, width = queries.shape
    heads_dev = width // DH
    lines, near, pair = (lax.axis_size(axis) for axis in SEQ)
    line, side, core = (lax.axis_index(axis) for axis in SEQ)
    column = lax.axis_index(HEAD) * heads_dev // GQA * DH

    def own(x):
        return lax.dynamic_slice_in_dim(x, column, DH, 1)

    kv = jnp.concatenate(
        [
            jnp.concatenate([own(cache_keys), own(new_keys)], axis=0),
            jnp.concatenate([own(cache_values), own(new_values)], axis=0),
        ],
        axis=1,
    )
    near_kv = lax.all_gather(lax.ppermute(kv, NEAR, [(0, 1), (1, 0)]), PAIR)
    kv = lax.all_gather(kv, PAIR)
    chips = [line * near + side, line * near + 1 - side]
    lens = jnp.concatenate(
        [lax.dynamic_slice_in_dim(cache_len, chip * pair, pair) for chip in chips]
    )
    key_pos = jnp.concatenate(
        [
            lax.dynamic_slice_in_dim(positions, chip * pair * tok_dev, pair * tok_dev)
            for chip in chips
        ]
    )[None, :]
    query_pos = lax.dynamic_index_in_dim(
        positions.reshape(lines, near * pair, tok_dev), side * pair + core, 1, keepdims=False
    ).reshape(lines * tok_dev, 1)

    partial_rows = attend(lens, key_pos, query_pos, sent_to_all(queries, LINE), kv, near_kv)
    attended = combine(lax.all_to_all(partial_rows, LINE, 0, 0, tiled=True))
    attended = sent_to_all(attended, (LINE, NEAR))
    other = lax.ppermute(attended, PAIR, [(0, 1), (1, 0)])
    first = core == 0
    attended = jnp.stack(
        [jnp.where(first, attended, other), jnp.where(first, other, attended)], axis=1
    )
    partial_out = jnp.dot(
        attended.reshape(-1, width), out_weight, preferred_element_type=F32
    ).astype(BF16)
    blocks = partial_out.reshape(lines * near * pair, tok_dev, -1)
    arrived = lax.all_to_all(blocks, PLANE, 0, 0, tiled=True)
    summed = jnp.sum(arrived.astype(F32), axis=0).astype(BF16)
    far = lax.ppermute(summed, FAR, [(0, 1), (1, 0)])
    whole = (summed.astype(F32) + far.astype(F32)).astype(BF16)
    return sent_to_all(whole, PLANE).reshape(partial_out.shape).astype(F32)


def solution(mesh):
    torus = Mesh(mesh.devices.reshape(4, 2, 2, 2, 4, 4), (*SEQ, *HEAD))
    return jax.shard_map(
        body,
        mesh=torus,
        in_specs=(
            P(SEQ, HEAD),
            P(SEQ, None),
            P(SEQ, None),
            P(SEQ, None),
            P(SEQ, None),
            P(),
            P(),
            P(HEAD, SEQ),
        ),
        out_specs=P(None, SEQ),
        check_vma=False,
    )
```

```python
import functools

import jax
import jax.numpy as jnp
from jax import lax
from jax.experimental import pallas as pl
from jax.experimental.pallas import tpu as pltpu
from jax.sharding import Mesh
from jax.sharding import PartitionSpec as P

DH = 128
GQA = 16
LINE = "line"
NEAR = "near"
PAIR = "core"
FAR = "far"
PLANE = ("x", "y")
SEQ = (LINE, NEAR, PAIR)
HEAD = (FAR, *PLANE)
HIDDEN = -1e30
SCALE = DH**-0.5 * 1.4426950408889634
BF16 = jnp.bfloat16
F32 = jnp.float32


def sent_to_all(x, axes):
    copies = jnp.broadcast_to(x, (lax.axis_size(axes), *x.shape))
    return lax.all_to_all(copies, axes, split_axis=0, concat_axis=0, tiled=True)


def attend_kernel(lens_ref, key_pos_ref, query_pos_ref, query_ref, kv_ref, near_kv_ref, out_ref):
    lines, rows, width = query_ref.shape
    heads = width // DH
    tokens = lines * rows
    slices = [ref.at[core] for ref in (kv_ref, near_kv_ref) for core in range(2)]
    stripe = kv_ref.shape[1] - key_pos_ref.shape[1] // len(slices)
    nt = (((1,), (1,)), ((), ()))
    slot = lax.broadcasted_iota(jnp.int32, (1, stripe), 1)
    live = [slot < lens_ref[i] for i in range(len(slices))]
    causal = key_pos_ref[...] <= query_pos_ref[...]
    new_keys = jnp.concatenate([ref[stripe:, :DH] for ref in slices], axis=0)
    new_values = jnp.concatenate([ref[stripe:, DH:] for ref in slices], axis=0)
    lane = lax.broadcasted_iota(jnp.int32, (tokens, DH), 1)
    stats = jnp.zeros((tokens, DH), F32)
    for head in range(heads):
        query = query_ref[:, :, head * DH : (head + 1) * DH].reshape(tokens, DH)
        parts = [
            jnp.where(
                shown,
                lax.dot_general(query, ref[:stripe, :DH], nt, preferred_element_type=F32),
                HIDDEN,
            )
            for shown, ref in zip(live, slices)
        ]
        parts.append(
            jnp.where(
                causal, lax.dot_general(query, new_keys, nt, preferred_element_type=F32), HIDDEN
            )
        )
        peak = functools.reduce(
            jnp.maximum, [jnp.max(part, axis=1, keepdims=True) for part in parts]
        )
        peak = peak.astype(BF16).astype(F32)
        expo = [jnp.exp2((part - peak) * SCALE) for part in parts]
        total = sum(jnp.sum(part, axis=1, keepdims=True) for part in expo)
        values = [ref[:stripe, DH:] for ref in slices] + [new_values]
        mixed = sum(
            jnp.dot(part.astype(BF16), value, preferred_element_type=F32)
            for part, value in zip(expo, values)
        )
        out_ref[:, :, head * DH : (head + 1) * DH] = mixed.astype(BF16).reshape(lines, rows, DH)
        coarse = total.astype(BF16).astype(F32)
        stats = jnp.where(lane == head, peak, stats)
        stats = jnp.where(lane == heads + head, coarse, stats)
        stats = jnp.where(lane == 2 * heads + head, total - coarse, stats)
    out_ref[:, :, width:] = stats.astype(BF16).reshape(lines, rows, DH)


def attend(lens, key_pos, query_pos, queries, kv, near_kv):
    lines, rows, width = queries.shape
    work = lines * rows * (width // DH) * 4 * kv.shape[1]
    vmem = pl.BlockSpec(memory_space=pltpu.VMEM)
    return pl.pallas_call(
        attend_kernel,
        out_shape=jax.ShapeDtypeStruct((lines, rows, width + DH), BF16),
        in_specs=[pl.BlockSpec(memory_space=pltpu.SMEM), vmem, vmem, vmem, vmem, vmem],
        out_specs=vmem,
        compiler_params=pltpu.CompilerParams(vmem_limit_bytes=40 << 20),
        cost_estimate=pl.CostEstimate(
            flops=4 * work * DH, transcendentals=work, bytes_accessed=4 * (queries.size + kv.size)
        ),
        name="attend",
    )(lens, key_pos, query_pos, queries, kv, near_kv)


def combine_kernel(part_ref, out_ref):
    width = out_ref.shape[1]
    heads = width // DH
    stats = part_ref[:, :, width:].astype(F32)
    for head in range(heads):
        peaks = stats[:, :, head : head + 1]
        sums = (
            stats[:, :, heads + head : heads + head + 1]
            + stats[:, :, 2 * heads + head : 2 * heads + head + 1]
        )
        scale = jnp.exp2((peaks - jnp.max(peaks, axis=0, keepdims=True)) * SCALE)
        scale = scale / jnp.sum(scale * sums, axis=0, keepdims=True)
        columns = slice(head * DH, (head + 1) * DH)
        mixed = jnp.sum(part_ref[:, :, columns].astype(F32) * scale, axis=0)
        out_ref[:, columns] = mixed.astype(BF16)


def combine(parts):
    lines, rows, width = parts.shape
    vmem = pl.BlockSpec(memory_space=pltpu.VMEM)
    return pl.pallas_call(
        combine_kernel,
        out_shape=jax.ShapeDtypeStruct((rows, width - DH), BF16),
        in_specs=[vmem],
        out_specs=vmem,
        compiler_params=pltpu.CompilerParams(vmem_limit_bytes=8 << 20),
        cost_estimate=pl.CostEstimate(
            flops=2 * parts.size, transcendentals=0, bytes_accessed=2 * parts.size
        ),
        name="combine",
    )(parts)


def swapped(x, axis, mask=1):
    return lax.ppermute(x, axis, [(i, i ^ mask) for i in range(lax.axis_size(axis))])


def after(x, *others):
    return lax.optimization_barrier((x, *others))[0]


def plane_groups():
    along_x = [[x * 4 + y for x in range(4)] for y in range(4)]
    along_y = [[x * 4 + y for y in range(4)] for x in range(4)]

    def both(even, odd):
        return even + [[16 + index for index in group] for group in odd]

    return both(along_x, along_y), both(along_y, along_x)


def exchanged(blocks, groups):
    return lax.all_to_all(blocks, (PAIR, *PLANE), 0, 0, axis_index_groups=groups, tiled=True)


def summed_on_arrival(blocks, groups):
    return jnp.sum(exchanged(blocks, groups).astype(F32), axis=0).astype(BF16)


def sent_within(x, groups):
    return exchanged(jnp.broadcast_to(x, (len(groups[0]), *x.shape)), groups)


def joined(x, axis, dim):
    other = swapped(x, axis)
    first = lax.axis_index(axis) == 0
    return jnp.stack([jnp.where(first, x, other), jnp.where(first, other, x)], axis=dim)


def body(queries, new_keys, new_values, cache_keys, cache_values, positions, cache_len, out_weight):
    tok_dev, width = queries.shape
    heads_dev = width // DH
    lines, near, pair = (lax.axis_size(axis) for axis in SEQ)
    line, side, core = (lax.axis_index(axis) for axis in SEQ)
    column = lax.axis_index(HEAD) * heads_dev // GQA * DH

    def own(x):
        return lax.dynamic_slice_in_dim(x, column, DH, 1)

    own_kv = jnp.concatenate(
        [
            jnp.concatenate([own(cache_keys), own(new_keys)], axis=0),
            jnp.concatenate([own(cache_values), own(new_values)], axis=0),
        ],
        axis=1,
    )
    near_kv = lax.all_gather(swapped(own_kv, NEAR), PAIR)
    kv = lax.all_gather(own_kv, PAIR)
    chips = [line * near + side, line * near + 1 - side]
    lens = jnp.concatenate(
        [lax.dynamic_slice_in_dim(cache_len, chip * pair, pair) for chip in chips]
    )
    key_pos = jnp.concatenate(
        [
            lax.dynamic_slice_in_dim(positions, chip * pair * tok_dev, pair * tok_dev)
            for chip in chips
        ]
    )[None, :]
    query_pos = lax.dynamic_index_in_dim(
        positions.reshape(lines, near * pair, tok_dev), side * pair + core, 1, keepdims=False
    ).reshape(lines * tok_dev, 1)
    everyone = sent_to_all(after(queries, own_kv), LINE)

    partial_rows = attend(lens, key_pos, query_pos, everyone, kv, near_kv)
    attended = combine(lax.all_to_all(partial_rows, LINE, 0, 0, tiled=True))
    attended = joined(sent_to_all(attended, (LINE, NEAR)), PAIR, 1).reshape(-1, width)
    partial_out = jnp.dot(attended, out_weight, preferred_element_type=F32).astype(BF16)
    first, second = plane_groups()
    blocks = partial_out.reshape(4, 4, tok_dev, -1)
    blocks = summed_on_arrival(summed_on_arrival(blocks, first), second)
    whole = (blocks.astype(F32) + swapped(blocks, FAR).astype(F32)).astype(BF16)
    whole = sent_within(sent_within(whole, second), first)
    return whole.reshape(partial_out.shape).astype(F32)


def solution(mesh):
    torus = Mesh(mesh.devices.reshape(4, 2, 2, 2, 4, 4), (*SEQ, *HEAD))
    return jax.shard_map(
        body,
        mesh=torus,
        in_specs=(
            P(SEQ, HEAD),
            P(SEQ, None),
            P(SEQ, None),
            P(SEQ, None),
            P(SEQ, None),
            P(),
            P(),
            P(HEAD, SEQ),
        ),
        out_specs=P(None, SEQ),
        check_vma=False,
    )
```

```python
import functools

import jax
import jax.numpy as jnp
from jax import lax
from jax.experimental import pallas as pl
from jax.experimental.pallas import tpu as pltpu
from jax.sharding import Mesh
from jax.sharding import PartitionSpec as P

DH = 128
GQA = 16
LINE = "line"
NEAR = "near"
PAIR = "core"
FAR = "far"
PLANE = ("x", "y")
SEQ = (LINE, NEAR, PAIR)
HEAD = (FAR, *PLANE)
HIDDEN = -1e30
SCALE = DH**-0.5 * 1.4426950408889634
BF16 = jnp.bfloat16
F32 = jnp.float32


def attend_kernel(lens_ref, key_pos_ref, query_pos_ref, query_ref, kv_ref, near_kv_ref, out_ref):
    lines, rows, width = query_ref.shape
    heads = width // DH
    tokens = lines * rows
    slices = [ref.at[core] for ref in (kv_ref, near_kv_ref) for core in range(2)]
    stripe = kv_ref.shape[1] - key_pos_ref.shape[1] // len(slices)
    nt = (((1,), (1,)), ((), ()))
    slot = lax.broadcasted_iota(jnp.int32, (1, stripe), 1)
    live = [slot < lens_ref[i] for i in range(len(slices))]
    causal = key_pos_ref[...] <= query_pos_ref[...]
    new_keys = jnp.concatenate([ref[stripe:, :DH] for ref in slices], axis=0)
    new_values = jnp.concatenate([ref[stripe:, DH:] for ref in slices], axis=0)
    lane = lax.broadcasted_iota(jnp.int32, (tokens, DH), 1)
    stats = jnp.zeros((tokens, DH), F32)
    for head in range(heads):
        query = query_ref[:, :, head * DH : (head + 1) * DH].reshape(tokens, DH)
        parts = [
            jnp.where(
                shown,
                lax.dot_general(query, ref[:stripe, :DH], nt, preferred_element_type=F32),
                HIDDEN,
            )
            for shown, ref in zip(live, slices)
        ]
        parts.append(
            jnp.where(
                causal, lax.dot_general(query, new_keys, nt, preferred_element_type=F32), HIDDEN
            )
        )
        peak = functools.reduce(
            jnp.maximum, [jnp.max(part, axis=1, keepdims=True) for part in parts]
        )
        peak = peak.astype(BF16).astype(F32)
        expo = [jnp.exp2((part - peak) * SCALE) for part in parts]
        total = sum(jnp.sum(part, axis=1, keepdims=True) for part in expo)
        values = [ref[:stripe, DH:] for ref in slices] + [new_values]
        mixed = sum(
            jnp.dot(part.astype(BF16), value, preferred_element_type=F32)
            for part, value in zip(expo, values)
        )
        out_ref[:, :, head * DH : (head + 1) * DH] = mixed.astype(BF16).reshape(lines, rows, DH)
        coarse = total.astype(BF16).astype(F32)
        stats = jnp.where(lane == head, peak, stats)
        stats = jnp.where(lane == heads + head, coarse, stats)
        stats = jnp.where(lane == 2 * heads + head, total - coarse, stats)
    out_ref[:, :, width:] = stats.astype(BF16).reshape(lines, rows, DH)


def attend(lens, key_pos, query_pos, queries, kv, near_kv):
    lines, rows, width = queries.shape
    work = lines * rows * (width // DH) * 4 * kv.shape[1]
    vmem = pl.BlockSpec(memory_space=pltpu.VMEM)
    return pl.pallas_call(
        attend_kernel,
        out_shape=jax.ShapeDtypeStruct((lines, rows, width + DH), BF16),
        in_specs=[pl.BlockSpec(memory_space=pltpu.SMEM), vmem, vmem, vmem, vmem, vmem],
        out_specs=vmem,
        compiler_params=pltpu.CompilerParams(vmem_limit_bytes=40 << 20),
        cost_estimate=pl.CostEstimate(
            flops=4 * work * DH, transcendentals=work, bytes_accessed=4 * (queries.size + kv.size)
        ),
        name="attend",
    )(lens, key_pos, query_pos, queries, kv, near_kv)


def combine_kernel(part_ref, out_ref):
    width = out_ref.shape[2]
    heads = width // DH
    stats = part_ref[:, :, width:].astype(F32)
    for head in range(heads):
        peaks = stats[:, :, head : head + 1]
        sums = (
            stats[:, :, heads + head : heads + head + 1]
            + stats[:, :, 2 * heads + head : 2 * heads + head + 1]
        )
        scale = jnp.exp2((peaks - jnp.max(peaks, axis=0, keepdims=True)) * SCALE)
        scale = scale / jnp.sum(scale * sums, axis=0, keepdims=True)
        columns = slice(head * DH, (head + 1) * DH)
        mixed = jnp.sum(part_ref[:, :, columns].astype(F32) * scale, axis=0)
        for copy in range(out_ref.shape[0]):
            out_ref[copy, :, columns] = mixed.astype(BF16)


def combine(parts):
    lines, rows, width = parts.shape
    vmem = pl.BlockSpec(memory_space=pltpu.VMEM)
    return pl.pallas_call(
        combine_kernel,
        out_shape=jax.ShapeDtypeStruct((lines, rows, width - DH), BF16),
        in_specs=[vmem],
        out_specs=vmem,
        compiler_params=pltpu.CompilerParams(vmem_limit_bytes=8 << 20),
        cost_estimate=pl.CostEstimate(
            flops=2 * parts.size, transcendentals=0, bytes_accessed=2 * parts.size
        ),
        name="combine",
    )(parts)


def swapped(x, axis, mask=1):
    return lax.ppermute(x, axis, [(i, i ^ mask) for i in range(lax.axis_size(axis))])


def moved_kernel(moves, *refs):
    *refs, sems = refs
    started = [
        pltpu.make_async_copy(source, target, sems.at[i])
        for i, (source, target) in enumerate(moves(*refs))
    ]
    for move in started:
        move.start()
    for move in started:
        move.wait()


def moved(moves, count, out_shape, *operands):
    size = 2 * out_shape.size
    return pl.pallas_call(
        functools.partial(moved_kernel, moves),
        out_shape=out_shape,
        in_specs=[
            pl.BlockSpec(memory_space=pltpu.SMEM if x.dtype == jnp.int32 else pl.ANY)
            for x in operands
        ],
        out_specs=pl.BlockSpec(memory_space=pltpu.VMEM),
        scratch_shapes=[pltpu.SemaphoreType.DMA((count,))],
        cost_estimate=pl.CostEstimate(flops=0, transcendentals=0, bytes_accessed=2 * size),
        name="moved",
    )(*operands)


def one_head(column, new_keys, new_values, cache_keys, cache_values):
    stripe, tokens = cache_keys.shape[0], new_keys.shape[0]

    def moves(column_ref, new_keys_ref, new_values_ref, keys_ref, values_ref, kv_ref):
        head = pl.ds(pl.multiple_of(column_ref[0], DH), DH)
        old, new = pl.ds(0, stripe), pl.ds(stripe, tokens)
        return [
            (keys_ref.at[:, head], kv_ref.at[old, pl.ds(0, DH)]),
            (values_ref.at[:, head], kv_ref.at[old, pl.ds(DH, DH)]),
            (new_keys_ref.at[:, head], kv_ref.at[new, pl.ds(0, DH)]),
            (new_values_ref.at[:, head], kv_ref.at[new, pl.ds(DH, DH)]),
        ]

    shape = jax.ShapeDtypeStruct((stripe + tokens, 2 * DH), BF16)
    return moved(moves, 4, shape, column[None], new_keys, new_values, cache_keys, cache_values)


def copied(x, count):
    def moves(x_ref, out_ref):
        return [(x_ref, out_ref.at[i]) for i in range(count)]

    return moved(moves, count, jax.ShapeDtypeStruct((count, *x.shape), x.dtype), x)


def plane_groups():
    along_x = [[x * 4 + y for x in range(4)] for y in range(4)]
    along_y = [[x * 4 + y for y in range(4)] for x in range(4)]

    def both(even, odd):
        return even + [[16 + index for index in group] for group in odd]

    return both(along_x, along_y), both(along_y, along_x)


def exchanged(blocks, groups):
    return lax.all_to_all(blocks, (PAIR, *PLANE), 0, 0, axis_index_groups=groups, tiled=True)


def summed_on_arrival(blocks, groups):
    return jnp.sum(exchanged(blocks, groups).astype(F32), axis=0).astype(BF16)


def sent_within(x, groups):
    return exchanged(jnp.broadcast_to(x, (len(groups[0]), *x.shape)), groups)


def joined(x, axis, dim):
    other = swapped(x, axis)
    first = lax.axis_index(axis) == 0
    return jnp.stack([jnp.where(first, x, other), jnp.where(first, other, x)], axis=dim)


def body(queries, new_keys, new_values, cache_keys, cache_values, positions, cache_len, out_weight):
    tok_dev, width = queries.shape
    heads_dev = width // DH
    lines, near, pair = (lax.axis_size(axis) for axis in SEQ)
    line, side, core = (lax.axis_index(axis) for axis in SEQ)
    column = lax.axis_index(HEAD) * heads_dev // GQA * DH

    own_kv = one_head(column, new_keys, new_values, cache_keys, cache_values)
    near_kv = lax.all_gather(swapped(own_kv, NEAR), PAIR)
    kv = lax.all_gather(own_kv, PAIR)
    chips = [line * near + side, line * near + 1 - side]
    lens = jnp.concatenate(
        [lax.dynamic_slice_in_dim(cache_len, chip * pair, pair) for chip in chips]
    )
    key_pos = jnp.concatenate(
        [
            lax.dynamic_slice_in_dim(positions, chip * pair * tok_dev, pair * tok_dev)
            for chip in chips
        ]
    )[None, :]
    query_pos = lax.dynamic_index_in_dim(
        positions.reshape(lines, near * pair, tok_dev), side * pair + core, 1, keepdims=False
    ).reshape(lines * tok_dev, 1)
    query, _ = lax.optimization_barrier((queries, own_kv))
    everyone = lax.all_to_all(copied(query, lines), LINE, 0, 0, tiled=True)
    partial_rows = attend(lens, key_pos, query_pos, everyone, kv, near_kv)
    attended = combine(lax.all_to_all(partial_rows, LINE, 0, 0, tiled=True))
    attended = lax.all_to_all(attended, LINE, 0, 0, tiled=True)
    attended = joined(joined(attended, NEAR, 1), PAIR, 2).reshape(-1, width)
    partial_out = jnp.dot(attended, out_weight, preferred_element_type=F32).astype(BF16)
    first, second = plane_groups()
    blocks = partial_out.reshape(4, 4, tok_dev, -1)
    blocks = summed_on_arrival(summed_on_arrival(blocks, first), second)
    whole = (blocks.astype(F32) + swapped(blocks, FAR).astype(F32)).astype(BF16)
    whole = sent_within(sent_within(whole, second), first)
    return whole.reshape(partial_out.shape).astype(F32)


def solution(mesh):
    torus = Mesh(mesh.devices.reshape(4, 2, 2, 2, 4, 4), (*SEQ, *HEAD))
    return jax.shard_map(
        body,
        mesh=torus,
        in_specs=(
            P(SEQ, HEAD),
            P(SEQ, None),
            P(SEQ, None),
            P(SEQ, None),
            P(SEQ, None),
            P(),
            P(),
            P(HEAD, SEQ),
        ),
        out_specs=P(None, SEQ),
        check_vma=False,
    )
```

```python
import functools

import jax
import jax.numpy as jnp
from jax import lax
from jax.experimental import pallas as pl
from jax.experimental.pallas import tpu as pltpu
from jax.sharding import Mesh
from jax.sharding import PartitionSpec as P

DH = 128
GQA = 16
LINE = "line"
NEAR = "near"
PAIR = "core"
FAR = "far"
PLANE = ("x", "y")
SEQ = (LINE, NEAR, PAIR)
HEAD = (FAR, *PLANE)
HIDDEN = -1e30
SCALE = DH**-0.5 * 1.4426950408889634
BF16 = jnp.bfloat16
F32 = jnp.float32


def packed(stats):
    groups = stats.shape[0] // 8
    return sum(
        pltpu.roll(stats[8 * i : 8 * (i + 1)], DH // groups * i, 1) for i in range(groups)
    )


def unpacked(tile, rows):
    groups = rows // 8
    return jnp.concatenate(
        [pltpu.roll(tile, (DH - DH // groups * i) % DH, 1) for i in range(groups)], axis=0
    )


def attend_kernel(own, scalars_ref, key_pos_ref, query_pos_ref, query_ref, kv_ref, near_kv_ref, *refs):
    *own_refs, out_ref = refs
    lines, rows, width = query_ref.shape
    heads = width // DH
    slices = [ref.at[core] for ref in (kv_ref, near_kv_ref) for core in range(2)]
    line = scalars_ref[len(slices)]
    taken = [0] if own else [lax.rem(line + i, lines) for i in range(1, lines)]
    tokens = len(taken) * rows
    stripe = kv_ref.shape[1] - key_pos_ref.shape[1] // len(slices)
    nt = (((1,), (1,)), ((), ()))
    slot = lax.broadcasted_iota(jnp.int32, (1, stripe), 1)
    live = [slot < scalars_ref[i] for i in range(len(slices))]
    query_pos = jnp.concatenate([query_pos_ref[i] for i in taken], axis=0)
    causal = key_pos_ref[...] <= query_pos
    new_keys = jnp.concatenate([ref[stripe:, :DH] for ref in slices], axis=0)
    new_values = jnp.concatenate([ref[stripe:, DH:] for ref in slices], axis=0)
    queries = jnp.concatenate([query_ref[i] for i in taken], axis=0)
    lane = lax.broadcasted_iota(jnp.int32, (tokens, DH), 1)
    stats = jnp.zeros((tokens, DH), F32)
    for head in range(heads):
        columns = slice(head * DH, (head + 1) * DH)
        query = queries[:, columns]
        parts = [
            jnp.where(
                shown,
                lax.dot_general(query, ref[:stripe, :DH], nt, preferred_element_type=F32),
                HIDDEN,
            )
            for shown, ref in zip(live, slices)
        ]
        parts.append(
            jnp.where(
                causal, lax.dot_general(query, new_keys, nt, preferred_element_type=F32), HIDDEN
            )
        )
        peak = functools.reduce(
            jnp.maximum, [jnp.max(part, axis=1, keepdims=True) for part in parts]
        )
        peak = peak.astype(BF16).astype(F32)
        expo = [jnp.exp2((part - peak) * SCALE) for part in parts]
        total = sum(jnp.sum(part, axis=1, keepdims=True) for part in expo)
        values = [ref[:stripe, DH:] for ref in slices] + [new_values]
        mixed = sum(
            jnp.dot(part.astype(BF16), value, preferred_element_type=F32)
            for part, value in zip(expo, values)
        ).astype(BF16)
        for i, block in enumerate(taken):
            out_ref[block, :rows, columns] = mixed[i * rows : (i + 1) * rows]
        coarse = total.astype(BF16).astype(F32)
        stats = jnp.where(lane == head, peak, stats)
        stats = jnp.where(lane == heads + head, coarse, stats)
        stats = jnp.where(lane == 2 * heads + head, total - coarse, stats)
    spare = jnp.zeros((8, width - DH), F32)
    for i, block in enumerate(taken):
        tile = jnp.concatenate([packed(stats[i * rows : (i + 1) * rows]), spare], axis=1)
        out_ref[block, rows:, :] = tile.astype(BF16)
    for own_ref in own_refs:
        out_ref[line] = own_ref[0]


def attend(scalars, key_pos, query_pos, queries, kv, near_kv, *own_rows):
    lines, rows, width = queries.shape
    work = max(1, lines - 1) * rows * (width // DH) * 4 * kv.shape[1]
    vmem = pl.BlockSpec(memory_space=pltpu.VMEM)
    return pl.pallas_call(
        functools.partial(attend_kernel, not own_rows),
        out_shape=jax.ShapeDtypeStruct((lines, rows + 8, width), BF16),
        in_specs=[pl.BlockSpec(memory_space=pltpu.SMEM)] + [vmem] * (5 + len(own_rows)),
        out_specs=vmem,
        compiler_params=pltpu.CompilerParams(vmem_limit_bytes=40 << 20),
        cost_estimate=pl.CostEstimate(
            flops=4 * work * DH, transcendentals=work, bytes_accessed=4 * (queries.size + kv.size)
        ),
        name="attend",
    )(scalars, key_pos, query_pos, queries, kv, near_kv, *own_rows)


def combine_kernel(part_ref, out_ref):
    copies, rows, width = out_ref.shape
    heads = width // DH
    stats = [
        unpacked(part_ref[i, rows:, :DH].astype(F32), rows) for i in range(part_ref.shape[0])
    ]
    for head in range(heads):
        columns = slice(head * DH, (head + 1) * DH)
        peaks = [stat[:, head : head + 1] for stat in stats]
        sums = [
            stat[:, heads + head : heads + head + 1] + stat[:, 2 * heads + head : 2 * heads + head + 1]
            for stat in stats
        ]
        top = functools.reduce(jnp.maximum, peaks)
        scales = [jnp.exp2((peak - top) * SCALE) for peak in peaks]
        inverse = 1.0 / sum(scale * part for scale, part in zip(scales, sums))
        mixed = sum(
            part_ref[i, :rows, columns].astype(F32) * (scale * inverse)
            for i, scale in enumerate(scales)
        ).astype(BF16)
        for copy in range(copies):
            out_ref[copy, :, columns] = mixed


def combine(parts):
    copies, rows, width = parts.shape
    vmem = pl.BlockSpec(memory_space=pltpu.VMEM)
    return pl.pallas_call(
        combine_kernel,
        out_shape=jax.ShapeDtypeStruct((copies, rows - 8, width), BF16),
        in_specs=[vmem],
        out_specs=vmem,
        compiler_params=pltpu.CompilerParams(vmem_limit_bytes=8 << 20),
        cost_estimate=pl.CostEstimate(
            flops=2 * parts.size, transcendentals=0, bytes_accessed=2 * parts.size
        ),
        name="combine",
    )(parts)


def swapped(x, axis, mask=1):
    return lax.ppermute(x, axis, [(i, i ^ mask) for i in range(lax.axis_size(axis))])


def moved_kernel(moves, *refs):
    *refs, sems = refs
    started = [
        pltpu.make_async_copy(source, target, sems.at[i])
        for i, (source, target) in enumerate(moves(*refs))
    ]
    for move in started:
        move.start()
    for move in started:
        move.wait()


def moved(moves, count, out_shape, *operands):
    size = 2 * out_shape.size
    return pl.pallas_call(
        functools.partial(moved_kernel, moves),
        out_shape=out_shape,
        in_specs=[
            pl.BlockSpec(memory_space=pltpu.SMEM if x.dtype == jnp.int32 else pl.ANY)
            for x in operands
        ],
        out_specs=pl.BlockSpec(memory_space=pltpu.VMEM),
        scratch_shapes=[pltpu.SemaphoreType.DMA((count,))],
        cost_estimate=pl.CostEstimate(flops=0, transcendentals=0, bytes_accessed=2 * size),
        name="moved",
    )(*operands)


def one_head(column, new_keys, new_values, cache_keys, cache_values):
    stripe, tokens = cache_keys.shape[0], new_keys.shape[0]

    def moves(column_ref, new_keys_ref, new_values_ref, keys_ref, values_ref, kv_ref):
        head = pl.ds(pl.multiple_of(column_ref[0], DH), DH)
        old, new = pl.ds(0, stripe), pl.ds(stripe, tokens)
        return [
            (keys_ref.at[:, head], kv_ref.at[old, pl.ds(0, DH)]),
            (values_ref.at[:, head], kv_ref.at[old, pl.ds(DH, DH)]),
            (new_keys_ref.at[:, head], kv_ref.at[new, pl.ds(0, DH)]),
            (new_values_ref.at[:, head], kv_ref.at[new, pl.ds(DH, DH)]),
        ]

    shape = jax.ShapeDtypeStruct((stripe + tokens, 2 * DH), BF16)
    return moved(moves, 4, shape, column[None], new_keys, new_values, cache_keys, cache_values)


def copied(x, count):
    def moves(x_ref, out_ref):
        return [(x_ref, out_ref.at[i]) for i in range(count)]

    return moved(moves, count, jax.ShapeDtypeStruct((count, *x.shape), x.dtype), x)


def plane_groups():
    along_x = [[x * 4 + y for x in range(4)] for y in range(4)]
    along_y = [[x * 4 + y for y in range(4)] for x in range(4)]

    def both(even, odd):
        return even + [[16 + index for index in group] for group in odd]

    return both(along_x, along_y), both(along_y, along_x)


def exchanged(blocks, groups):
    return lax.all_to_all(blocks, (PAIR, *PLANE), 0, 0, axis_index_groups=groups, tiled=True)


def summed_on_arrival(blocks, groups):
    return jnp.sum(exchanged(blocks, groups).astype(F32), axis=0).astype(BF16)


def sent_within(x, groups):
    return exchanged(jnp.broadcast_to(x, (len(groups[0]), *x.shape)), groups)


def joined(x, axis, dim):
    other = swapped(x, axis)
    first = lax.axis_index(axis) == 0
    return jnp.stack([jnp.where(first, x, other), jnp.where(first, other, x)], axis=dim)


def body(queries, new_keys, new_values, cache_keys, cache_values, positions, cache_len, out_weight):
    tok_dev, width = queries.shape
    heads_dev = width // DH
    lines, near, pair = (lax.axis_size(axis) for axis in SEQ)
    line, side, core = (lax.axis_index(axis) for axis in SEQ)
    column = lax.axis_index(HEAD) * heads_dev // GQA * DH

    own_kv = one_head(column, new_keys, new_values, cache_keys, cache_values)
    near_kv = lax.all_gather(swapped(own_kv, NEAR), PAIR)
    kv = lax.all_gather(own_kv, PAIR)
    chips = [line * near + side, line * near + 1 - side]
    scalars = jnp.concatenate(
        [lax.dynamic_slice_in_dim(cache_len, chip * pair, pair) for chip in chips] + [line[None]]
    )
    key_pos = jnp.concatenate(
        [
            lax.dynamic_slice_in_dim(positions, chip * pair * tok_dev, pair * tok_dev)
            for chip in chips
        ]
    )[None, :]
    query_pos = lax.dynamic_index_in_dim(
        positions.reshape(lines, near * pair, tok_dev), side * pair + core, 1, keepdims=False
    )[:, :, None]
    query, _ = lax.optimization_barrier((queries, own_kv))
    everyone = lax.all_to_all(copied(query, lines), LINE, 0, 0, tiled=True)
    own_pos = lax.dynamic_slice_in_dim(query_pos, line, 1)
    own_rows = attend(scalars, key_pos, own_pos, queries[None], kv, near_kv)
    partial_rows = attend(scalars, key_pos, query_pos, everyone, kv, near_kv, own_rows)
    attended = combine(lax.all_to_all(partial_rows, LINE, 0, 0, tiled=True))
    attended = lax.all_to_all(attended, LINE, 0, 0, tiled=True)
    attended = joined(joined(attended, NEAR, 1), PAIR, 2).reshape(-1, width)
    partial_out = jnp.dot(attended, out_weight, preferred_element_type=F32).astype(BF16)
    first, second = plane_groups()
    blocks = partial_out.reshape(4, 4, tok_dev, -1)
    blocks = summed_on_arrival(summed_on_arrival(blocks, first), second)
    whole = (blocks.astype(F32) + swapped(blocks, FAR).astype(F32)).astype(BF16)
    whole = sent_within(sent_within(whole, second), first)
    return whole.reshape(partial_out.shape).astype(F32)


def solution(mesh):
    torus = Mesh(mesh.devices.reshape(4, 2, 2, 2, 4, 4), (*SEQ, *HEAD))
    return jax.shard_map(
        body,
        mesh=torus,
        in_specs=(
            P(SEQ, HEAD),
            P(SEQ, None),
            P(SEQ, None),
            P(SEQ, None),
            P(SEQ, None),
            P(),
            P(),
            P(HEAD, SEQ),
        ),
        out_specs=P(None, SEQ),
        check_vma=False,
    )
```

```python
import functools

import jax
import jax.numpy as jnp
from jax import lax
from jax.experimental import pallas as pl
from jax.experimental.pallas import tpu as pltpu
from jax.sharding import Mesh
from jax.sharding import PartitionSpec as P

DH = 128
GQA = 16
LINE = "line"
NEAR = "near"
PAIR = "core"
FAR = "far"
PLANE = ("x", "y")
SEQ = (LINE, NEAR, PAIR)
HEAD = (FAR, *PLANE)
HIDDEN = -1e30
SCALE = DH**-0.5 * 1.4426950408889634
BF16 = jnp.bfloat16
F32 = jnp.float32


def packed(stats):
    groups = stats.shape[0] // 8
    return sum(
        pltpu.roll(stats[8 * i : 8 * (i + 1)], DH // groups * i, 1) for i in range(groups)
    )


def unpacked(tile, rows):
    groups = rows // 8
    return jnp.concatenate(
        [pltpu.roll(tile, (DH - DH // groups * i) % DH, 1) for i in range(groups)], axis=0
    )


def attend_kernel(own, scalars_ref, key_pos_ref, query_pos_ref, query_ref, kv_ref, near_kv_ref, *refs):
    *own_refs, out_ref = refs
    lines, rows, width = query_ref.shape
    heads = width // DH
    slices = [ref.at[core] for ref in (kv_ref, near_kv_ref) for core in range(2)]
    line = scalars_ref[len(slices)]
    taken = [0] if own else [lax.rem(line + i, lines) for i in range(1, lines)]
    tokens = len(taken) * rows
    stripe = kv_ref.shape[1] - key_pos_ref.shape[1] // len(slices)
    nt = (((1,), (1,)), ((), ()))
    slot = lax.broadcasted_iota(jnp.int32, (1, stripe), 1)
    live = [slot < scalars_ref[i] for i in range(len(slices))]
    query_pos = jnp.concatenate([query_pos_ref[i] for i in taken], axis=0)
    causal = key_pos_ref[...] <= query_pos
    new_keys = jnp.concatenate([ref[stripe:, :DH] for ref in slices], axis=0)
    new_values = jnp.concatenate([ref[stripe:, DH:] for ref in slices], axis=0)
    queries = jnp.concatenate([query_ref[i] for i in taken], axis=0)
    lane = lax.broadcasted_iota(jnp.int32, (tokens, DH), 1)
    stats = jnp.zeros((tokens, DH), F32)
    for head in range(heads):
        columns = slice(head * DH, (head + 1) * DH)
        query = queries[:, columns]
        parts = [
            jnp.where(
                shown,
                lax.dot_general(query, ref[:stripe, :DH], nt, preferred_element_type=F32),
                HIDDEN,
            )
            for shown, ref in zip(live, slices)
        ]
        parts.append(
            jnp.where(
                causal, lax.dot_general(query, new_keys, nt, preferred_element_type=F32), HIDDEN
            )
        )
        peak = functools.reduce(
            jnp.maximum, [jnp.max(part, axis=1, keepdims=True) for part in parts]
        )
        peak = peak.astype(BF16).astype(F32)
        expo = [jnp.exp2((part - peak) * SCALE) for part in parts]
        total = sum(jnp.sum(part, axis=1, keepdims=True) for part in expo)
        values = [ref[:stripe, DH:] for ref in slices] + [new_values]
        mixed = sum(
            jnp.dot(part.astype(BF16), value, preferred_element_type=F32)
            for part, value in zip(expo, values)
        ).astype(BF16)
        for i, block in enumerate(taken):
            out_ref[block, :rows, columns] = mixed[i * rows : (i + 1) * rows]
        coarse = total.astype(BF16).astype(F32)
        stats = jnp.where(lane == head, peak, stats)
        stats = jnp.where(lane == heads + head, coarse, stats)
        stats = jnp.where(lane == 2 * heads + head, total - coarse, stats)
    spare = jnp.zeros((8, width - DH), F32)
    for i, block in enumerate(taken):
        tile = jnp.concatenate([packed(stats[i * rows : (i + 1) * rows]), spare], axis=1)
        out_ref[block, rows:, :] = tile.astype(BF16)
    for own_ref in own_refs:
        out_ref[line] = own_ref[0]


def attend(scalars, key_pos, query_pos, queries, kv, near_kv, *own_rows):
    lines, rows, width = queries.shape
    work = max(1, lines - 1) * rows * (width // DH) * 4 * kv.shape[1]
    vmem = pl.BlockSpec(memory_space=pltpu.VMEM)
    return pl.pallas_call(
        functools.partial(attend_kernel, not own_rows),
        out_shape=jax.ShapeDtypeStruct((lines, rows + 8, width), BF16),
        in_specs=[pl.BlockSpec(memory_space=pltpu.SMEM)] + [vmem] * (5 + len(own_rows)),
        out_specs=vmem,
        compiler_params=pltpu.CompilerParams(vmem_limit_bytes=40 << 20),
        cost_estimate=pl.CostEstimate(
            flops=4 * work * DH, transcendentals=work, bytes_accessed=4 * (queries.size + kv.size)
        ),
        name="attend",
    )(scalars, key_pos, query_pos, queries, kv, near_kv, *own_rows)


def combine_kernel(part_ref, out_ref):
    copies, rows, width = out_ref.shape
    heads = width // DH
    stats = [
        unpacked(part_ref[i, rows:, :DH].astype(F32), rows) for i in range(part_ref.shape[0])
    ]
    for head in range(heads):
        columns = slice(head * DH, (head + 1) * DH)
        peaks = [stat[:, head : head + 1] for stat in stats]
        sums = [
            stat[:, heads + head : heads + head + 1] + stat[:, 2 * heads + head : 2 * heads + head + 1]
            for stat in stats
        ]
        top = functools.reduce(jnp.maximum, peaks)
        scales = [jnp.exp2((peak - top) * SCALE) for peak in peaks]
        inverse = 1.0 / sum(scale * part for scale, part in zip(scales, sums))
        mixed = sum(
            part_ref[i, :rows, columns].astype(F32) * (scale * inverse)
            for i, scale in enumerate(scales)
        ).astype(BF16)
        for copy in range(copies):
            out_ref[copy, :, columns] = mixed


def combine(parts):
    copies, rows, width = parts.shape
    vmem = pl.BlockSpec(memory_space=pltpu.VMEM)
    return pl.pallas_call(
        combine_kernel,
        out_shape=jax.ShapeDtypeStruct((copies, rows - 8, width), BF16),
        in_specs=[vmem],
        out_specs=vmem,
        compiler_params=pltpu.CompilerParams(vmem_limit_bytes=8 << 20),
        cost_estimate=pl.CostEstimate(
            flops=2 * parts.size, transcendentals=0, bytes_accessed=2 * parts.size
        ),
        name="combine",
    )(parts)


def swapped(x, axis, mask=1):
    return lax.ppermute(x, axis, [(i, i ^ mask) for i in range(lax.axis_size(axis))])


def moved_kernel(moves, *refs):
    *refs, sems = refs
    started = [
        pltpu.make_async_copy(source, target, sems.at[i])
        for i, (source, target) in enumerate(moves(*refs))
    ]
    for move in started:
        move.start()
    for move in started:
        move.wait()


def moved(moves, count, out_shape, *operands):
    size = 2 * out_shape.size
    return pl.pallas_call(
        functools.partial(moved_kernel, moves),
        out_shape=out_shape,
        in_specs=[
            pl.BlockSpec(memory_space=pltpu.SMEM if x.dtype == jnp.int32 else pl.ANY)
            for x in operands
        ],
        out_specs=pl.BlockSpec(memory_space=pltpu.VMEM),
        scratch_shapes=[pltpu.SemaphoreType.DMA((count,))],
        cost_estimate=pl.CostEstimate(flops=0, transcendentals=0, bytes_accessed=2 * size),
        name="moved",
    )(*operands)


def one_head(column, new_keys, new_values, cache_keys, cache_values):
    stripe, tokens = cache_keys.shape[0], new_keys.shape[0]

    def moves(column_ref, new_keys_ref, new_values_ref, keys_ref, values_ref, kv_ref):
        head = pl.ds(pl.multiple_of(column_ref[0], DH), DH)
        old, new = pl.ds(0, stripe), pl.ds(stripe, tokens)
        return [
            (keys_ref.at[:, head], kv_ref.at[old, pl.ds(0, DH)]),
            (values_ref.at[:, head], kv_ref.at[old, pl.ds(DH, DH)]),
            (new_keys_ref.at[:, head], kv_ref.at[new, pl.ds(0, DH)]),
            (new_values_ref.at[:, head], kv_ref.at[new, pl.ds(DH, DH)]),
        ]

    shape = jax.ShapeDtypeStruct((stripe + tokens, 2 * DH), BF16)
    return moved(moves, 4, shape, column[None], new_keys, new_values, cache_keys, cache_values)


def copied(x, count):
    def moves(x_ref, out_ref):
        return [(x_ref, out_ref.at[i]) for i in range(count)]

    return moved(moves, count, jax.ShapeDtypeStruct((count, *x.shape), x.dtype), x)


def widened_kernel(x_ref, out_ref, wide_ref, sems):
    steps = sems.shape[0]
    step = x_ref.shape[0] // steps
    moves = []
    for i in range(steps):
        taken = pl.ds(i * step, step)
        wide_ref[taken, :] = x_ref[taken, :].astype(F32)
        moves.append(pltpu.make_async_copy(wide_ref.at[taken], out_ref.at[taken], sems.at[i]))
        moves[-1].start()
    for move in moves:
        move.wait()


def widened(x, steps=8):
    return pl.pallas_call(
        widened_kernel,
        out_shape=jax.ShapeDtypeStruct(x.shape, F32),
        in_specs=[pl.BlockSpec(memory_space=pltpu.VMEM)],
        out_specs=pl.BlockSpec(memory_space=pl.ANY),
        scratch_shapes=[pltpu.VMEM(x.shape, F32), pltpu.SemaphoreType.DMA((steps,))],
        compiler_params=pltpu.CompilerParams(vmem_limit_bytes=8 << 20),
        cost_estimate=pl.CostEstimate(flops=0, transcendentals=0, bytes_accessed=6 * x.size),
        name="widened",
    )(x)


def summed_kernel(x_ref, out_ref):
    for block in range(out_ref.shape[0]):
        total = sum(x_ref[i, block].astype(F32) for i in range(x_ref.shape[0]))
        out_ref[block] = total.astype(BF16)


def summed(x):
    vmem = pl.BlockSpec(memory_space=pltpu.VMEM)
    return pl.pallas_call(
        summed_kernel,
        out_shape=jax.ShapeDtypeStruct(x.shape[1:], BF16),
        in_specs=[vmem],
        out_specs=vmem,
        compiler_params=pltpu.CompilerParams(vmem_limit_bytes=8 << 20),
        cost_estimate=pl.CostEstimate(flops=x.size, transcendentals=0, bytes_accessed=3 * x.size),
        name="summed",
    )(x)


def plane_groups():
    along_x = [[x * 4 + y for x in range(4)] for y in range(4)]
    along_y = [[x * 4 + y for y in range(4)] for x in range(4)]

    def both(even, odd):
        return even + [[16 + index for index in group] for group in odd]

    return both(along_x, along_y), both(along_y, along_x)


def exchanged(blocks, groups):
    return lax.all_to_all(blocks, (PAIR, *PLANE), 0, 0, axis_index_groups=groups, tiled=True)


def summed_on_arrival(blocks, groups):
    return jnp.sum(exchanged(blocks, groups).astype(F32), axis=0).astype(BF16)


def sent_within(x, groups):
    return exchanged(jnp.broadcast_to(x, (len(groups[0]), *x.shape)), groups)


def joined(x, axis, dim):
    other = swapped(x, axis)
    first = lax.axis_index(axis) == 0
    return jnp.stack([jnp.where(first, x, other), jnp.where(first, other, x)], axis=dim)


def body(queries, new_keys, new_values, cache_keys, cache_values, positions, cache_len, out_weight):
    tok_dev, width = queries.shape
    heads_dev = width // DH
    lines, near, pair = (lax.axis_size(axis) for axis in SEQ)
    line, side, core = (lax.axis_index(axis) for axis in SEQ)
    column = lax.axis_index(HEAD) * heads_dev // GQA * DH

    own_kv = one_head(column, new_keys, new_values, cache_keys, cache_values)
    near_kv = lax.all_gather(swapped(own_kv, NEAR), PAIR)
    kv = lax.all_gather(own_kv, PAIR)
    chips = [line * near + side, line * near + 1 - side]
    scalars = jnp.concatenate(
        [lax.dynamic_slice_in_dim(cache_len, chip * pair, pair) for chip in chips] + [line[None]]
    )
    key_pos = jnp.concatenate(
        [
            lax.dynamic_slice_in_dim(positions, chip * pair * tok_dev, pair * tok_dev)
            for chip in chips
        ]
    )[None, :]
    query_pos = lax.dynamic_index_in_dim(
        positions.reshape(lines, near * pair, tok_dev), side * pair + core, 1, keepdims=False
    )[:, :, None]
    query, _ = lax.optimization_barrier((queries, own_kv))
    everyone = lax.all_to_all(copied(query, lines), LINE, 0, 0, tiled=True)
    own_pos = lax.dynamic_slice_in_dim(query_pos, line, 1)
    own_rows = attend(scalars, key_pos, own_pos, queries[None], kv, near_kv)
    partial_rows = attend(scalars, key_pos, query_pos, everyone, kv, near_kv, own_rows)
    attended = combine(lax.all_to_all(partial_rows, LINE, 0, 0, tiled=True))
    attended = lax.all_to_all(attended, LINE, 0, 0, tiled=True)
    attended = joined(joined(attended, NEAR, 1), PAIR, 2).reshape(-1, width)
    partial_out = jnp.dot(attended, out_weight, preferred_element_type=F32).astype(BF16)
    first, second = plane_groups()
    blocks = partial_out.reshape(4, 4, tok_dev, -1)
    blocks = summed_on_arrival(summed(exchanged(blocks, first)), second)
    whole = (blocks.astype(F32) + swapped(blocks, FAR).astype(F32)).astype(BF16)
    whole = sent_within(sent_within(whole, second), first)
    return widened(whole.reshape(partial_out.shape))


def solution(mesh):
    torus = Mesh(mesh.devices.reshape(4, 2, 2, 2, 4, 4), (*SEQ, *HEAD))
    return jax.shard_map(
        body,
        mesh=torus,
        in_specs=(
            P(SEQ, HEAD),
            P(SEQ, None),
            P(SEQ, None),
            P(SEQ, None),
            P(SEQ, None),
            P(),
            P(),
            P(HEAD, SEQ),
        ),
        out_specs=P(None, SEQ),
        check_vma=False,
    )
```

```python
import functools

import jax
import jax.numpy as jnp
from jax import lax
from jax.experimental import pallas as pl
from jax.experimental.pallas import tpu as pltpu
from jax.sharding import Mesh
from jax.sharding import PartitionSpec as P

DH = 128
GQA = 16
LINE = "line"
NEAR = "near"
PAIR = "core"
FAR = "far"
PLANE = ("x", "y")
SEQ = (LINE, NEAR, PAIR)
HEAD = (FAR, *PLANE)
HIDDEN = -1e30
SCALE = DH**-0.5 * 1.4426950408889634
BF16 = jnp.bfloat16
F32 = jnp.float32


def packed(stats):
    groups = stats.shape[0] // 8
    return sum(
        pltpu.roll(stats[8 * i : 8 * (i + 1)], DH // groups * i, 1) for i in range(groups)
    )


def unpacked(tile, rows):
    groups = rows // 8
    return jnp.concatenate(
        [pltpu.roll(tile, (DH - DH // groups * i) % DH, 1) for i in range(groups)], axis=0
    )


def attend_kernel(own, scalars_ref, key_pos_ref, query_pos_ref, query_ref, kv_ref, near_kv_ref, *refs):
    *own_refs, out_ref = refs
    lines, rows, width = query_ref.shape
    heads = width // DH
    slices = [ref.at[core] for ref in (kv_ref, near_kv_ref) for core in range(2)]
    line = scalars_ref[len(slices)]
    taken = [0] if own else [lax.rem(line + i, lines) for i in range(1, lines)]
    tokens = len(taken) * rows
    stripe = kv_ref.shape[1] - key_pos_ref.shape[1] // len(slices)
    nt = (((1,), (1,)), ((), ()))
    slot = lax.broadcasted_iota(jnp.int32, (1, stripe), 1)
    live = [slot < scalars_ref[i] for i in range(len(slices))]
    query_pos = jnp.concatenate([query_pos_ref[i] for i in taken], axis=0)
    causal = key_pos_ref[...] <= query_pos
    new_keys = jnp.concatenate([ref[stripe:, :DH] for ref in slices], axis=0)
    new_values = jnp.concatenate([ref[stripe:, DH:] for ref in slices], axis=0)
    queries = jnp.concatenate([query_ref[i] for i in taken], axis=0)
    lane = lax.broadcasted_iota(jnp.int32, (tokens, DH), 1)
    stats = jnp.zeros((tokens, DH), F32)
    for head in range(heads):
        columns = slice(head * DH, (head + 1) * DH)
        query = queries[:, columns]
        parts = [
            jnp.where(
                shown,
                lax.dot_general(query, ref[:stripe, :DH], nt, preferred_element_type=F32),
                HIDDEN,
            )
            for shown, ref in zip(live, slices)
        ]
        parts.append(
            jnp.where(
                causal, lax.dot_general(query, new_keys, nt, preferred_element_type=F32), HIDDEN
            )
        )
        peak = functools.reduce(
            jnp.maximum, [jnp.max(part, axis=1, keepdims=True) for part in parts]
        )
        peak = peak.astype(BF16).astype(F32)
        expo = [jnp.exp2((part - peak) * SCALE) for part in parts]
        total = sum(jnp.sum(part, axis=1, keepdims=True) for part in expo)
        values = [ref[:stripe, DH:] for ref in slices] + [new_values]
        mixed = sum(
            jnp.dot(part.astype(BF16), value, preferred_element_type=F32)
            for part, value in zip(expo, values)
        ).astype(BF16)
        for i, block in enumerate(taken):
            out_ref[block, :rows, columns] = mixed[i * rows : (i + 1) * rows]
        coarse = total.astype(BF16).astype(F32)
        stats = jnp.where(lane == head, peak, stats)
        stats = jnp.where(lane == heads + head, coarse, stats)
        stats = jnp.where(lane == 2 * heads + head, total - coarse, stats)
    spare = jnp.zeros((8, width - DH), F32)
    for i, block in enumerate(taken):
        tile = jnp.concatenate([packed(stats[i * rows : (i + 1) * rows]), spare], axis=1)
        out_ref[block, rows:, :] = tile.astype(BF16)
    for own_ref in own_refs:
        out_ref[line] = own_ref[0]


def attend(scalars, key_pos, query_pos, queries, kv, near_kv, *own_rows):
    lines, rows, width = queries.shape
    work = max(1, lines - 1) * rows * (width // DH) * 4 * kv.shape[1]
    vmem = pl.BlockSpec(memory_space=pltpu.VMEM)
    return pl.pallas_call(
        functools.partial(attend_kernel, not own_rows),
        out_shape=jax.ShapeDtypeStruct((lines, rows + 8, width), BF16),
        in_specs=[pl.BlockSpec(memory_space=pltpu.SMEM)] + [vmem] * (5 + len(own_rows)),
        out_specs=vmem,
        compiler_params=pltpu.CompilerParams(vmem_limit_bytes=40 << 20),
        cost_estimate=pl.CostEstimate(
            flops=4 * work * DH, transcendentals=work, bytes_accessed=4 * (queries.size + kv.size)
        ),
        name="attend",
    )(scalars, key_pos, query_pos, queries, kv, near_kv, *own_rows)


def combine_kernel(part_ref, out_ref):
    copies, rows, width = out_ref.shape
    heads = width // DH
    stats = [
        unpacked(part_ref[i, rows:, :DH].astype(F32), rows) for i in range(part_ref.shape[0])
    ]
    for head in range(heads):
        columns = slice(head * DH, (head + 1) * DH)
        peaks = [stat[:, head : head + 1] for stat in stats]
        sums = [
            stat[:, heads + head : heads + head + 1] + stat[:, 2 * heads + head : 2 * heads + head + 1]
            for stat in stats
        ]
        top = functools.reduce(jnp.maximum, peaks)
        scales = [jnp.exp2((peak - top) * SCALE) for peak in peaks]
        inverse = 1.0 / sum(scale * part for scale, part in zip(scales, sums))
        mixed = sum(
            part_ref[i, :rows, columns].astype(F32) * (scale * inverse)
            for i, scale in enumerate(scales)
        ).astype(BF16)
        for copy in range(copies):
            out_ref[copy, :, columns] = mixed


def combine(parts):
    copies, rows, width = parts.shape
    vmem = pl.BlockSpec(memory_space=pltpu.VMEM)
    return pl.pallas_call(
        combine_kernel,
        out_shape=jax.ShapeDtypeStruct((copies, rows - 8, width), BF16),
        in_specs=[vmem],
        out_specs=vmem,
        compiler_params=pltpu.CompilerParams(vmem_limit_bytes=8 << 20),
        cost_estimate=pl.CostEstimate(
            flops=2 * parts.size, transcendentals=0, bytes_accessed=2 * parts.size
        ),
        name="combine",
    )(parts)


def swapped(x, axis, mask=1):
    return lax.ppermute(x, axis, [(i, i ^ mask) for i in range(lax.axis_size(axis))])


def moved_kernel(moves, *refs):
    *refs, sems = refs
    started = [
        pltpu.make_async_copy(source, target, sems.at[i])
        for i, (source, target) in enumerate(moves(*refs))
    ]
    for move in started:
        move.start()
    for move in started:
        move.wait()


def moved(moves, count, out_shape, *operands):
    size = 2 * out_shape.size
    return pl.pallas_call(
        functools.partial(moved_kernel, moves),
        out_shape=out_shape,
        in_specs=[
            pl.BlockSpec(memory_space=pltpu.SMEM if x.dtype == jnp.int32 else pl.ANY)
            for x in operands
        ],
        out_specs=pl.BlockSpec(memory_space=pltpu.VMEM),
        scratch_shapes=[pltpu.SemaphoreType.DMA((count,))],
        cost_estimate=pl.CostEstimate(flops=0, transcendentals=0, bytes_accessed=2 * size),
        name="moved",
    )(*operands)


def one_head(column, new_keys, new_values, cache_keys, cache_values):
    stripe, tokens = cache_keys.shape[0], new_keys.shape[0]

    def moves(column_ref, new_keys_ref, new_values_ref, keys_ref, values_ref, kv_ref):
        head = pl.ds(pl.multiple_of(column_ref[0], DH), DH)
        old, new = pl.ds(0, stripe), pl.ds(stripe, tokens)
        return [
            (keys_ref.at[:, head], kv_ref.at[old, pl.ds(0, DH)]),
            (values_ref.at[:, head], kv_ref.at[old, pl.ds(DH, DH)]),
            (new_keys_ref.at[:, head], kv_ref.at[new, pl.ds(0, DH)]),
            (new_values_ref.at[:, head], kv_ref.at[new, pl.ds(DH, DH)]),
        ]

    shape = jax.ShapeDtypeStruct((stripe + tokens, 2 * DH), BF16)
    return moved(moves, 4, shape, column[None], new_keys, new_values, cache_keys, cache_values)


def copied(x, count):
    def moves(x_ref, out_ref):
        return [(x_ref, out_ref.at[i]) for i in range(count)]

    return moved(moves, count, jax.ShapeDtypeStruct((count, *x.shape), x.dtype), x)


def widened_kernel(x_ref, out_ref, wide_ref, sems):
    steps = sems.shape[0]
    step = x_ref.shape[0] // steps
    moves = []
    for i in range(steps):
        taken = pl.ds(i * step, step)
        wide_ref[taken, :] = x_ref[taken, :].astype(F32)
        moves.append(pltpu.make_async_copy(wide_ref.at[taken], out_ref.at[taken], sems.at[i]))
        moves[-1].start()
    for move in moves:
        move.wait()


def widened(x, steps=8):
    return pl.pallas_call(
        widened_kernel,
        out_shape=jax.ShapeDtypeStruct(x.shape, F32),
        in_specs=[pl.BlockSpec(memory_space=pltpu.VMEM)],
        out_specs=pl.BlockSpec(memory_space=pl.ANY),
        scratch_shapes=[pltpu.VMEM(x.shape, F32), pltpu.SemaphoreType.DMA((steps,))],
        compiler_params=pltpu.CompilerParams(vmem_limit_bytes=8 << 20),
        cost_estimate=pl.CostEstimate(flops=0, transcendentals=0, bytes_accessed=6 * x.size),
        name="widened",
    )(x)


def summed_kernel(x_ref, out_ref):
    for block in range(out_ref.shape[0]):
        total = sum(x_ref[i, block].astype(F32) for i in range(x_ref.shape[0]))
        out_ref[block] = total.astype(BF16)


def summed(x):
    vmem = pl.BlockSpec(memory_space=pltpu.VMEM)
    return pl.pallas_call(
        summed_kernel,
        out_shape=jax.ShapeDtypeStruct(x.shape[1:], BF16),
        in_specs=[vmem],
        out_specs=vmem,
        compiler_params=pltpu.CompilerParams(vmem_limit_bytes=8 << 20),
        cost_estimate=pl.CostEstimate(flops=x.size, transcendentals=0, bytes_accessed=3 * x.size),
        name="summed",
    )(x)


def plane_groups():
    along_x = [[x * 4 + y for x in range(4)] for y in range(4)]
    along_y = [[x * 4 + y for y in range(4)] for x in range(4)]

    def both(even, odd):
        return even + [[16 + index for index in group] for group in odd]

    return both(along_x, along_y), both(along_y, along_x)


def exchanged(blocks, groups):
    return lax.all_to_all(blocks, (PAIR, *PLANE), 0, 0, axis_index_groups=groups, tiled=True)


def summed_on_arrival(blocks, groups):
    return jnp.sum(exchanged(blocks, groups).astype(F32), axis=0).astype(BF16)


def sent_within(x, groups):
    return exchanged(jnp.broadcast_to(x, (len(groups[0]), *x.shape)), groups)


def ordered(x, other, axis, dim):
    first = lax.axis_index(axis) == 0
    return jnp.stack([jnp.where(first, x, other), jnp.where(first, other, x)], axis=dim)


def joined(x, axis, dim):
    return ordered(x, swapped(x, axis), axis, dim)


def body(queries, new_keys, new_values, cache_keys, cache_values, positions, cache_len, out_weight):
    tok_dev, width = queries.shape
    heads_dev = width // DH
    lines, near, pair = (lax.axis_size(axis) for axis in SEQ)
    line, side, core = (lax.axis_index(axis) for axis in SEQ)
    column = lax.axis_index(HEAD) * heads_dev // GQA * DH

    own_kv = one_head(column, new_keys, new_values, cache_keys, cache_values)
    near_kv = lax.all_gather(swapped(own_kv, NEAR), PAIR)
    kv = lax.all_gather(own_kv, PAIR)
    chips = [line * near + side, line * near + 1 - side]
    scalars = jnp.concatenate(
        [lax.dynamic_slice_in_dim(cache_len, chip * pair, pair) for chip in chips] + [line[None]]
    )
    key_pos = jnp.concatenate(
        [
            lax.dynamic_slice_in_dim(positions, chip * pair * tok_dev, pair * tok_dev)
            for chip in chips
        ]
    )[None, :]
    query_pos = lax.dynamic_index_in_dim(
        positions.reshape(lines, near * pair, tok_dev), side * pair + core, 1, keepdims=False
    )[:, :, None]
    query, _ = lax.optimization_barrier((queries, own_kv))
    everyone = lax.all_to_all(copied(query, lines), LINE, 0, 0, tiled=True)
    own_pos = lax.dynamic_slice_in_dim(query_pos, line, 1)
    own_rows = attend(scalars, key_pos, own_pos, queries[None], kv, near_kv)
    partial_rows = attend(scalars, key_pos, query_pos, everyone, kv, near_kv, own_rows)
    attended = combine(lax.all_to_all(partial_rows, LINE, 0, 0, tiled=True))
    attended = lax.all_to_all(attended, LINE, 0, 0, tiled=True)
    neighbour = swapped(attended, NEAR)
    attended, neighbour = joined(attended, PAIR, 1), joined(neighbour, PAIR, 1)
    attended = ordered(attended, neighbour, NEAR, 1).reshape(-1, width)
    partial_out = jnp.dot(attended, out_weight, preferred_element_type=F32).astype(BF16)
    first, second = plane_groups()
    blocks = partial_out.reshape(4, 4, tok_dev, -1)
    blocks = summed_on_arrival(summed(exchanged(blocks, first)), second)
    whole = (blocks.astype(F32) + swapped(blocks, FAR).astype(F32)).astype(BF16)
    whole = sent_within(sent_within(whole, second), first)
    return widened(whole.reshape(partial_out.shape))


def solution(mesh):
    torus = Mesh(mesh.devices.reshape(4, 2, 2, 2, 4, 4), (*SEQ, *HEAD))
    return jax.shard_map(
        body,
        mesh=torus,
        in_specs=(
            P(SEQ, HEAD),
            P(SEQ, None),
            P(SEQ, None),
            P(SEQ, None),
            P(SEQ, None),
            P(),
            P(),
            P(HEAD, SEQ),
        ),
        out_specs=P(None, SEQ),
        check_vma=False,
    )
```

```python
import functools

import jax
import jax.numpy as jnp
from jax import lax
from jax.experimental import pallas as pl
from jax.experimental.pallas import tpu as pltpu
from jax.sharding import Mesh
from jax.sharding import PartitionSpec as P

DH = 128
GQA = 16
LINE = "line"
NEAR = "near"
PAIR = "core"
FAR = "far"
PLANE = ("x", "y")
SEQ = (LINE, NEAR, PAIR)
HEAD = (FAR, *PLANE)
HIDDEN = -1e30
SCALE = DH**-0.5 * 1.4426950408889634
BF16 = jnp.bfloat16
F32 = jnp.float32


def packed(stats):
    groups = stats.shape[0] // 8
    return sum(
        pltpu.roll(stats[8 * i : 8 * (i + 1)], DH // groups * i, 1) for i in range(groups)
    )


def unpacked(tile, rows):
    groups = rows // 8
    return jnp.concatenate(
        [pltpu.roll(tile, (DH - DH // groups * i) % DH, 1) for i in range(groups)], axis=0
    )


def attend_kernel(own, scalars_ref, key_pos_ref, query_pos_ref, query_ref, kv_ref, near_kv_ref, *refs):
    *own_refs, out_ref = refs
    lines, rows, width = query_ref.shape
    heads = width // DH
    slices = [ref.at[core] for ref in (kv_ref, near_kv_ref) for core in range(2)]
    line = scalars_ref[len(slices)]
    taken = [0] if own else [lax.rem(line + i, lines) for i in range(1, lines)]
    tokens = len(taken) * rows
    stripe = kv_ref.shape[1] - key_pos_ref.shape[1] // len(slices)
    nt = (((1,), (1,)), ((), ()))
    slot = lax.broadcasted_iota(jnp.int32, (1, stripe), 1)
    live = [slot < scalars_ref[i] for i in range(len(slices))]
    query_pos = jnp.concatenate([query_pos_ref[i] for i in taken], axis=0)
    causal = key_pos_ref[...] <= query_pos
    new_keys = jnp.concatenate([ref[stripe:, :DH] for ref in slices], axis=0)
    new_values = jnp.concatenate([ref[stripe:, DH:] for ref in slices], axis=0)
    queries = jnp.concatenate([query_ref[i] for i in taken], axis=0)
    lane = lax.broadcasted_iota(jnp.int32, (tokens, DH), 1)
    stats = jnp.zeros((tokens, DH), F32)
    for head in range(heads):
        columns = slice(head * DH, (head + 1) * DH)
        query = queries[:, columns]
        parts = [
            jnp.where(
                shown,
                lax.dot_general(query, ref[:stripe, :DH], nt, preferred_element_type=F32),
                HIDDEN,
            )
            for shown, ref in zip(live, slices)
        ]
        parts.append(
            jnp.where(
                causal, lax.dot_general(query, new_keys, nt, preferred_element_type=F32), HIDDEN
            )
        )
        peak = functools.reduce(
            jnp.maximum, [jnp.max(part, axis=1, keepdims=True) for part in parts]
        )
        peak = peak.astype(BF16).astype(F32)
        expo = [jnp.exp2((part - peak) * SCALE) for part in parts]
        total = sum(jnp.sum(part, axis=1, keepdims=True) for part in expo)
        values = [ref[:stripe, DH:] for ref in slices] + [new_values]
        mixed = sum(
            jnp.dot(part.astype(BF16), value, preferred_element_type=F32)
            for part, value in zip(expo, values)
        ).astype(BF16)
        for i, block in enumerate(taken):
            out_ref[block, :rows, columns] = mixed[i * rows : (i + 1) * rows]
        coarse = total.astype(BF16).astype(F32)
        stats = jnp.where(lane == head, peak, stats)
        stats = jnp.where(lane == heads + head, coarse, stats)
        stats = jnp.where(lane == 2 * heads + head, total - coarse, stats)
    spare = jnp.zeros((8, width - DH), F32)
    for i, block in enumerate(taken):
        tile = jnp.concatenate([packed(stats[i * rows : (i + 1) * rows]), spare], axis=1)
        out_ref[block, rows:, :] = tile.astype(BF16)
    for own_ref in own_refs:
        out_ref[line] = own_ref[0]


def attend(scalars, key_pos, query_pos, queries, kv, near_kv, *own_rows):
    lines, rows, width = queries.shape
    work = max(1, lines - 1) * rows * (width // DH) * 4 * kv.shape[1]
    vmem = pl.BlockSpec(memory_space=pltpu.VMEM)
    return pl.pallas_call(
        functools.partial(attend_kernel, not own_rows),
        out_shape=jax.ShapeDtypeStruct((lines, rows + 8, width), BF16),
        in_specs=[pl.BlockSpec(memory_space=pltpu.SMEM)] + [vmem] * (5 + len(own_rows)),
        out_specs=vmem,
        compiler_params=pltpu.CompilerParams(vmem_limit_bytes=40 << 20),
        cost_estimate=pl.CostEstimate(
            flops=4 * work * DH, transcendentals=work, bytes_accessed=4 * (queries.size + kv.size)
        ),
        name="attend",
    )(scalars, key_pos, query_pos, queries, kv, near_kv, *own_rows)


def combine_kernel(part_ref, out_ref):
    copies, rows, width = out_ref.shape
    heads = width // DH
    stats = [
        unpacked(part_ref[i, rows:, :DH].astype(F32), rows) for i in range(part_ref.shape[0])
    ]
    for head in range(heads):
        columns = slice(head * DH, (head + 1) * DH)
        peaks = [stat[:, head : head + 1] for stat in stats]
        sums = [
            stat[:, heads + head : heads + head + 1] + stat[:, 2 * heads + head : 2 * heads + head + 1]
            for stat in stats
        ]
        top = functools.reduce(jnp.maximum, peaks)
        scales = [jnp.exp2((peak - top) * SCALE) for peak in peaks]
        inverse = 1.0 / sum(scale * part for scale, part in zip(scales, sums))
        mixed = sum(
            part_ref[i, :rows, columns].astype(F32) * (scale * inverse)
            for i, scale in enumerate(scales)
        ).astype(BF16)
        for copy in range(copies):
            out_ref[copy, :, columns] = mixed


def combine(parts):
    copies, rows, width = parts.shape
    vmem = pl.BlockSpec(memory_space=pltpu.VMEM)
    return pl.pallas_call(
        combine_kernel,
        out_shape=jax.ShapeDtypeStruct((copies, rows - 8, width), BF16),
        in_specs=[vmem],
        out_specs=vmem,
        compiler_params=pltpu.CompilerParams(vmem_limit_bytes=8 << 20),
        cost_estimate=pl.CostEstimate(
            flops=2 * parts.size, transcendentals=0, bytes_accessed=2 * parts.size
        ),
        name="combine",
    )(parts)


def swapped(x, axis, mask=1):
    return lax.ppermute(x, axis, [(i, i ^ mask) for i in range(lax.axis_size(axis))])


def moved_kernel(moves, *refs):
    *refs, sems = refs
    started = [
        pltpu.make_async_copy(source, target, sems.at[i])
        for i, (source, target) in enumerate(moves(*refs))
    ]
    for move in started:
        move.start()
    for move in started:
        move.wait()


def moved(moves, count, out_shape, *operands):
    size = 2 * out_shape.size
    return pl.pallas_call(
        functools.partial(moved_kernel, moves),
        out_shape=out_shape,
        in_specs=[
            pl.BlockSpec(memory_space=pltpu.SMEM if x.dtype == jnp.int32 else pl.ANY)
            for x in operands
        ],
        out_specs=pl.BlockSpec(memory_space=pltpu.VMEM),
        scratch_shapes=[pltpu.SemaphoreType.DMA((count,))],
        cost_estimate=pl.CostEstimate(flops=0, transcendentals=0, bytes_accessed=2 * size),
        name="moved",
    )(*operands)


def one_head(column, new_keys, new_values, cache_keys, cache_values):
    stripe, tokens = cache_keys.shape[0], new_keys.shape[0]

    def moves(column_ref, new_keys_ref, new_values_ref, keys_ref, values_ref, kv_ref):
        head = pl.ds(pl.multiple_of(column_ref[0], DH), DH)
        old, new = pl.ds(0, stripe), pl.ds(stripe, tokens)
        return [
            (keys_ref.at[:, head], kv_ref.at[old, pl.ds(0, DH)]),
            (values_ref.at[:, head], kv_ref.at[old, pl.ds(DH, DH)]),
            (new_keys_ref.at[:, head], kv_ref.at[new, pl.ds(0, DH)]),
            (new_values_ref.at[:, head], kv_ref.at[new, pl.ds(DH, DH)]),
        ]

    shape = jax.ShapeDtypeStruct((stripe + tokens, 2 * DH), BF16)
    return moved(moves, 4, shape, column[None], new_keys, new_values, cache_keys, cache_values)


def copied(x, count):
    def moves(x_ref, out_ref):
        return [(x_ref, out_ref.at[i]) for i in range(count)]

    return moved(moves, count, jax.ShapeDtypeStruct((count, *x.shape), x.dtype), x)


def widened_kernel(x_ref, out_ref, wide_ref, sems):
    steps = sems.shape[0]
    step = x_ref.shape[0] // steps
    moves = []
    for i in range(steps):
        taken = pl.ds(i * step, step)
        wide_ref[taken, :] = x_ref[taken, :].astype(F32)
        moves.append(pltpu.make_async_copy(wide_ref.at[taken], out_ref.at[taken], sems.at[i]))
        moves[-1].start()
    for move in moves:
        move.wait()


def widened(x, steps=16):
    return pl.pallas_call(
        widened_kernel,
        out_shape=jax.ShapeDtypeStruct(x.shape, F32),
        in_specs=[pl.BlockSpec(memory_space=pltpu.VMEM)],
        out_specs=pl.BlockSpec(memory_space=pl.ANY),
        scratch_shapes=[pltpu.VMEM(x.shape, F32), pltpu.SemaphoreType.DMA((steps,))],
        compiler_params=pltpu.CompilerParams(vmem_limit_bytes=8 << 20),
        cost_estimate=pl.CostEstimate(flops=0, transcendentals=0, bytes_accessed=6 * x.size),
        name="widened",
    )(x)


def summed_kernel(x_ref, out_ref):
    for block in range(out_ref.shape[0]):
        total = sum(x_ref[i, block].astype(F32) for i in range(x_ref.shape[0]))
        out_ref[block] = total.astype(BF16)


def summed(x):
    vmem = pl.BlockSpec(memory_space=pltpu.VMEM)
    return pl.pallas_call(
        summed_kernel,
        out_shape=jax.ShapeDtypeStruct(x.shape[1:], BF16),
        in_specs=[vmem],
        out_specs=vmem,
        compiler_params=pltpu.CompilerParams(vmem_limit_bytes=8 << 20),
        cost_estimate=pl.CostEstimate(flops=x.size, transcendentals=0, bytes_accessed=3 * x.size),
        name="summed",
    )(x)


def plane_groups():
    along_x = [[x * 4 + y for x in range(4)] for y in range(4)]
    along_y = [[x * 4 + y for y in range(4)] for x in range(4)]

    def both(even, odd):
        return even + [[16 + index for index in group] for group in odd]

    return both(along_x, along_y), both(along_y, along_x)


def exchanged(blocks, groups):
    return lax.all_to_all(blocks, (PAIR, *PLANE), 0, 0, axis_index_groups=groups, tiled=True)


def summed_on_arrival(blocks, groups):
    return jnp.sum(exchanged(blocks, groups).astype(F32), axis=0).astype(BF16)


def sent_within(x, groups):
    return exchanged(jnp.broadcast_to(x, (len(groups[0]), *x.shape)), groups)


def ordered(x, other, axis, dim):
    first = lax.axis_index(axis) == 0
    return jnp.stack([jnp.where(first, x, other), jnp.where(first, other, x)], axis=dim)


def joined(x, axis, dim):
    return ordered(x, swapped(x, axis), axis, dim)


def body(queries, new_keys, new_values, cache_keys, cache_values, positions, cache_len, out_weight):
    tok_dev, width = queries.shape
    heads_dev = width // DH
    lines, near, pair = (lax.axis_size(axis) for axis in SEQ)
    line, side, core = (lax.axis_index(axis) for axis in SEQ)
    column = lax.axis_index(HEAD) * heads_dev // GQA * DH

    own_kv = one_head(column, new_keys, new_values, cache_keys, cache_values)
    near_kv = lax.all_gather(swapped(own_kv, NEAR), PAIR)
    kv = lax.all_gather(own_kv, PAIR)
    chips = [line * near + side, line * near + 1 - side]
    scalars = jnp.concatenate(
        [lax.dynamic_slice_in_dim(cache_len, chip * pair, pair) for chip in chips] + [line[None]]
    )
    key_pos = jnp.concatenate(
        [
            lax.dynamic_slice_in_dim(positions, chip * pair * tok_dev, pair * tok_dev)
            for chip in chips
        ]
    )[None, :]
    query_pos = lax.dynamic_index_in_dim(
        positions.reshape(lines, near * pair, tok_dev), side * pair + core, 1, keepdims=False
    )[:, :, None]
    query, _ = lax.optimization_barrier((queries, own_kv))
    everyone = lax.all_to_all(copied(query, lines), LINE, 0, 0, tiled=True)
    own_pos = lax.dynamic_slice_in_dim(query_pos, line, 1)
    own_rows = attend(scalars, key_pos, own_pos, queries[None], kv, near_kv)
    partial_rows = attend(scalars, key_pos, query_pos, everyone, kv, near_kv, own_rows)
    attended = combine(lax.all_to_all(partial_rows, LINE, 0, 0, tiled=True))
    attended = lax.all_to_all(attended, LINE, 0, 0, tiled=True)
    neighbour = swapped(attended, NEAR)
    attended, neighbour = joined(attended, PAIR, 1), joined(neighbour, PAIR, 1)
    attended = ordered(attended, neighbour, NEAR, 1).reshape(-1, width)
    partial_out = jnp.dot(attended, out_weight, preferred_element_type=F32).astype(BF16)
    first, second = plane_groups()
    blocks = partial_out.reshape(4, 4, tok_dev, -1)
    blocks = summed_on_arrival(summed(exchanged(blocks, first)), second)
    whole = (blocks.astype(F32) + swapped(blocks, FAR).astype(F32)).astype(BF16)
    whole = sent_within(sent_within(whole, second), first)
    return widened(whole.reshape(partial_out.shape))


def solution(mesh):
    torus = Mesh(mesh.devices.reshape(4, 2, 2, 2, 4, 4), (*SEQ, *HEAD))
    return jax.shard_map(
        body,
        mesh=torus,
        in_specs=(
            P(SEQ, HEAD),
            P(SEQ, None),
            P(SEQ, None),
            P(SEQ, None),
            P(SEQ, None),
            P(),
            P(),
            P(HEAD, SEQ),
        ),
        out_specs=P(None, SEQ),
        check_vma=False,
    )
```
